32 devices in a mesh: dp: 16 (over z, y, x), cls: 2 (over core).
Axes of the slice: x: 2, y: 2, z: 4, core: 2. Of those that a mesh axis runs over, the one named last changes fastest.
Arguments:
- features: bfloat16 [3072, 2048], P('dp'), may hold values from -128 to 128
- labels: int32 [3072], P('dp'), may hold values from 0 to 16383
- weight: bfloat16 [2048, 16384], P('dp', 'cls'), may hold values from -1 to 1
- noise: float32 [16, 2, 1024, 1024], P('dp', 'cls'), may hold values from -6 to 6
Outputs:
- noisy_grad: float32 [16, 2, 1024, 1024], P('dp', 'cls')
The draws below stay inside these ranges and needn't reach their ends.
All inputs are finite; a program needn't handle non-finite values.
Results may differ from the reference program's by a relative error of at most 0.0017.
Values may be sent and summed in bfloat16 or wider, within the bound.
A program may use at most 128 MiB of HBM per device.

```python
import math
import jax
import jax.numpy as jnp
import numpy as np
from jax import lax

D = 2048
CLASSES = 16384
CSPLIT = 8
TOKENS = 3072
DSPLIT = 2
DBLK = 1024
CBLK = 1024
N_DP = 16
N_CLS = 2


def draw_features(key, part):
    subkeys = jax.random.split(jax.random.fold_in(key, 11), 3)
    row_scale = jnp.exp(jax.random.uniform(subkeys[0], (TOKENS, 1), jnp.float32, math.log(0.1), math.log(10.0)))
    col_scale = jnp.exp(jax.random.uniform(subkeys[1], (1, D), jnp.float32, math.log(0.3), math.log(3.0)))
    values = row_scale * col_scale * jnp.clip(jax.random.normal(subkeys[2], (TOKENS, D), jnp.float32), -4.0, 4.0)
    return values.astype(jnp.bfloat16)


def draw_weight(key, part):
    subkeys = jax.random.split(jax.random.fold_in(key, 13), 1)
    values = jnp.clip(jax.random.normal(subkeys[0], (D, CLASSES), jnp.float32), -4.0, 4.0) / math.sqrt(D)
    return values.astype(jnp.bfloat16)


def place_ends(values, key, least, high):
    longest = values.shape.index(max(values.shape))
    spots = []
    for shift in (0, 1):
        where = [jax.random.randint(jax.random.fold_in(key, axis), (), 0, length) for axis, length in enumerate(values.shape)]
        where[longest] = (where[longest] + shift) % values.shape[longest]
        spots.append(tuple(where))
    return values.at[spots[0]].set(least).at[spots[1]].set(high)


def shard_levels(rng, shape, cuts, smallest, high):
    def one(position, shards_of):
        steps = jax.random.uniform(jax.random.fold_in(jax.random.fold_in(rng, 6), position), (shards_of,), jnp.float32, smallest / len(cuts), high / len(cuts))
        return jnp.repeat(jnp.exp(steps), shape[position] // shards_of).reshape((-1,) + (1,) * (len(shape) - position - 1))

    gain = one(*cuts[0])
    for cut in cuts[1:]:
        gain = gain * one(*cut)
    return gain


def rank_table(amount, lean):
    loads = [(1 << 20) // math.isqrt(standing ** lean) + 1 for standing in range(1, amount + 1)]
    scale = 1 + sum(loads) // (1 << 30)
    return np.cumsum(np.array([max(1, weight // scale) for weight in loads]))


def ranked_ids(own_key, dims, amount, slope):
    listing = rank_table(amount, slope)
    ticket = jax.random.randint(jax.random.fold_in(own_key, 1), dims, 0, int(listing[amount - 1]))
    grade = jnp.searchsorted(jnp.asarray(listing, jnp.int32), ticket, side="right")
    return jax.random.permutation(jax.random.fold_in(own_key, 2), amount)[grade].astype(jnp.int32)


def centred(rng, extent, deviation, bound, cuts=(), kind=jnp.bfloat16):
    entries = deviation * jax.random.normal(rng, extent, jnp.float32)
    if cuts:
        entries = entries * shard_levels(rng, extent, cuts, -0.22, 0.18)
    return jnp.clip(entries, -bound, bound).astype(kind)


def setup_inputs(seed: int = 0) -> dict:
    streams_of = jax.random.split(jax.random.key(seed), 5)
    features = draw_features(jax.random.fold_in(streams_of[4], 71), 0)
    labels = place_ends(ranked_ids(streams_of[1], (TOKENS,), CLASSES, 1), jax.random.fold_in(streams_of[1], 3), 0, CLASSES - 1).astype(jnp.int32)
    weight = draw_weight(jax.random.fold_in(streams_of[4], 71), 0)
    noise = centred(streams_of[3], (N_DP, N_CLS, DBLK, CBLK), 1.0, 6.0, ((0, 16), (1, 2)), jnp.float32)
    return {"features": features, "labels": labels, "weight": weight, "noise": noise}


CLIP_NORM = 40.0
NOISE_STD = 0.4

def reference(features, labels, weight, noise):
    block_rows = math.gcd(TOKENS, 512)
    count = TOKENS // block_rows
    feat_blocks = features.reshape(count, block_rows, D)
    label_blocks = labels.reshape(count, block_rows)

    def step_block(accum, pair):
        feat_block, label_block = pair
        logits = jnp.dot(feat_block, weight, preferred_element_type=jnp.float32)
        row_max = lax.optimization_barrier(jnp.max(logits, axis=1))
        exponent = jnp.exp(logits - row_max[:, None])
        row_total = lax.optimization_barrier(jnp.sum(exponent, axis=1))
        row_square = lax.optimization_barrier(jnp.sum(exponent * exponent, axis=1))
        label_hit = lax.broadcasted_iota(jnp.int32, logits.shape, 1) == label_block.astype(jnp.int32)[:, None]
        onehot = label_hit.astype(logits.dtype)
        picked = lax.optimization_barrier(jnp.sum(onehot * logits, axis=1))
        energy = lax.optimization_barrier(jnp.sum(jnp.square(feat_block.astype(jnp.float32)), axis=1))
        spread = row_square / (row_total * row_total) - 2.0 * jnp.exp(picked - row_max) / row_total + 1.0
        factor = CLIP_NORM * lax.rsqrt(jnp.maximum(energy * spread, CLIP_NORM * CLIP_NORM))
        softmax = exponent / row_total[:, None]
        weighted = (factor[:, None] * (softmax - onehot)).astype(jnp.bfloat16)
        accum = accum + lax.dot_general(feat_block, weighted, (((0,), (0,)), ((), ())), preferred_element_type=jnp.float32)
        return (accum, None)
    gradient, _ = lax.scan(step_block, jnp.zeros((D, CLASSES), jnp.float32), (feat_blocks, label_blocks))
    blocked = gradient.reshape(DSPLIT, DBLK, N_CLS, CSPLIT, CBLK).transpose(0, 3, 2, 1, 4).reshape(N_DP, N_CLS, DBLK, CBLK)
    return blocked + NOISE_STD * noise
```

```python
import functools

import jax
import jax.numpy as jnp
from jax import lax
from jax.experimental import pallas as pl
from jax.experimental.pallas import tpu as pltpu
from jax.sharding import PartitionSpec as P

CSPLIT = 8
CLIP_NORM = 40.0
NOISE_STD = 0.4
CHUNKS = 4
PLANE = 4
LANES = 128
MESH = pl.DeviceIdType.MESH


def head_kernel(n_dp, n_cls, feat_ref, label_ref, weight_ref, noise_ref, out_ref,
                feats, turned_feats, wcols, wstage, exps, grads, coefs, sides, label_cols, marks, maxima, scale_cols,
                stats, all_stats, finals, all_finals,
                fsend, frecv, bsend, brecv, psend, precv, zsend, zrecv, lsend, lrecv, tsend, trecv, gsend, grecv,
                local_sem, noise_sem, out_sem):
    f32 = jnp.float32
    me = lax.axis_index("dp")
    cls = lax.axis_index("cls")
    sibling = 1 - cls
    stages = 4
    half, depth = feats.shape[2:]
    chunks, _, depth_block, width = wcols.shape
    cols = chunks * width
    row_block = turned_feats.shape[0]
    count = CSPLIT * n_cls
    place = me % CSPLIT * n_cls + cls
    level = me // PLANE
    spot = me % PLANE

    def group_peer(hop):
        there = (place + hop) % count
        return (me // CSPLIT * CSPLIT + there // n_cls, there % n_cls)

    barrier = pltpu.get_barrier_semaphore()
    for hop in range(1, n_dp):
        pl.semaphore_signal(barrier, inc=1, device_id=((me + hop) % n_dp, cls), device_id_type=MESH)
    for hop in range(1, count):
        pl.semaphore_signal(barrier, inc=1, device_id=group_peer(hop), device_id_type=MESH)
    pl.semaphore_wait(barrier, n_dp - 1 + count - 1)

    bit_step = [(1 << b) * (1 - 2 * ((me // (1 << b)) % 2)) for b in range(stages)]

    def flip(mask):
        return sum(bit_step[b] for b in range(stages) if mask >> b & 1)

    def stage_steps(which):
        return [bit_step[3], bit_step[2],
                bit_step[1] * (1 - which) + bit_step[0] * which,
                bit_step[0] * (1 - which) + bit_step[1] * which]

    steps = stage_steps(cls)
    sib_steps = stage_steps(sibling)

    def origin(mask, table):
        there = me
        for s in range(stages):
            if mask >> s & 1:
                there = there + table[s]
        return there

    sends = []

    def push(source, target, out_sem, in_sem, device):
        copy = pltpu.make_async_remote_copy(
            src_ref=source, dst_ref=target, send_sem=out_sem, recv_sem=in_sem,
            device_id=device, device_id_type=MESH,
        )
        copy.start()
        return copy

    def arrived(ref, sem):
        pltpu.make_async_remote_copy(
            src_ref=ref, dst_ref=ref, send_sem=sem, recv_sem=sem,
            device_id=(me, sibling), device_id_type=MESH,
        ).wait_recv()

    own_half = feat_ref.at[pl.ds(pl.multiple_of(cls * half, half), half)]

    def feat_forward(mask, first, last):
        source = feats.at[cls, origin(mask, steps)] if mask else own_half
        for s in range(max(mask.bit_length(), first), last):
            sends.append(push(source, feats.at[cls, origin(mask, steps)], fsend.at[mask * stages + s],
                              frecv.at[mask | 1 << s], (me + steps[s], cls)))

    def feat_share(mask):
        block = feats.at[cls, origin(mask, steps)]
        sends.append(push(block, block, bsend.at[mask], brecv.at[mask], (me, sibling)))

    def feat_step(mask):
        arrived(feats.at[cls, origin(mask, steps)], frecv.at[mask])
        feat_forward(mask, 0, stages)
        feat_share(mask)

    parity = level % 2

    def block_cols(side, there, c):
        return pl.ds(pl.multiple_of((side * PLANE + there) * cols + c * width, width), width)

    def plane_send(c):
        for r in range(1, PLANE):
            peer = me + flip(r)
            at = c * 2 * PLANE + r * 2
            sends.append(push(weight_ref.at[:, block_cols(parity, peer % PLANE, c)], wcols.at[c, me],
                              psend.at[at], precv.at[at], (peer, cls)))
            sends.append(push(weight_ref.at[:, block_cols(1 - parity, peer % PLANE, c)], wstage.at[c, r],
                              psend.at[at + 1], precv.at[at + 1], (peer, cls)))

    def column_send(c, r, kept):
        if r:
            at = c * 2 * PLANE + r * 2
            arrived(wcols.at[c, me + flip(r)], precv.at[at])
            arrived(wstage.at[c, r], precv.at[at + 1])
        for m in (2, 3, 1):
            if r:
                source = wcols.at[c, me + flip(r)] if m == 2 else wstage.at[c, r]
            else:
                source = weight_ref.at[:, block_cols(parity if m == 2 else 1 - parity, spot, c)]
            at = (c * PLANE + r) * PLANE + m
            kept.append(push(source, wcols.at[c, me + flip(r)], zsend.at[at], zrecv.at[at],
                             (me + flip(m * PLANE), cls)))

    feat_forward(0, 0, 2)
    for c in range(chunks):
        plane_send(c)
    column = [[] for _ in range(chunks)]
    column_send(0, 0, column[0])
    keep = [pltpu.make_async_copy(feat_ref.at[pl.ds(h * half, half)], feats.at[h, me], local_sem.at[h])
            for h in range(2)]
    keep += [pltpu.make_async_copy(weight_ref.at[:, block_cols(parity, spot, c)], wcols.at[c, me], local_sem.at[2 + c])
             for c in range(chunks)]
    for copy in keep:
        copy.start()
    noise_copies = [
        pltpu.make_async_copy(noise_ref.at[:, pl.ds(c * width, width)], grads.at[c], noise_sem.at[c])
        for c in range(chunks)]
    sides[me] = label_ref[...]
    for hop in range(1, n_dp):
        sends.append(push(sides.at[me], sides.at[me], lsend.at[hop], lrecv.at[hop], ((me + hop) % n_dp, cls)))

    for r in range(1, PLANE):
        column_send(0, r, column[0])
    feat_forward(0, 2, stages)
    for r in range(PLANE):
        column_send(1, r, column[1])
    feat_step(1)
    feat_step(2)
    feat_step(3)
    for copy in noise_copies:
        copy.start()
    for copy in column[0]:
        copy.wait_send()
    for r in range(PLANE):
        column_send(2, r, column[2])
    for mask in range(4, 8):
        feat_step(mask)
    for copy in column[1]:
        copy.wait_send()
    for r in range(PLANE):
        column_send(3, r, column[3])
    for mask in range(8, 16):
        feat_step(mask)
    for mask in range(1, 16):
        arrived(feats.at[sibling, origin(mask, sib_steps)], brecv.at[mask])

    for hop in range(1, n_dp):
        arrived(sides.at[(me + n_dp - hop) % n_dp], lrecv.at[hop])
    for copy in keep:
        copy.wait()

    for h in range(2):
        rows = jnp.concatenate([sides[i, :, h * LANES:(h + 1) * LANES] for i in range(n_dp)], axis=0).astype(f32)
        label_cols[h] = jnp.concatenate([rows, jnp.zeros((LANES - n_dp, LANES), f32)], axis=0).T[0:half]

    first_row = pl.multiple_of(me // CSPLIT * row_block, row_block)
    quad = LANES // 32

    def turn_body(t, carry):
        h, k = t // (n_dp // quad), t % (n_dp // quad)
        part = feats[h, pl.ds(k * quad, quad), :, pl.ds(first_row, row_block)].reshape(quad * half, row_block)
        turned_feats[:, pl.ds(pl.multiple_of(t * quad * half, LANES), quad * half)] = part.T
        return carry

    lax.fori_loop(0, 2 * n_dp // quad, turn_body, 0)

    lane = lax.broadcasted_iota(jnp.int32, (half, LANES), 1)
    energy_cols = jnp.zeros((half, LANES), f32)
    for h in range(2):
        value = feats[h, place].astype(f32)
        energy_cols = jnp.where(lane == h, jnp.sum(value * value, axis=1, keepdims=True), energy_cols)
    energy_rows = jnp.concatenate([energy_cols, jnp.zeros((LANES - half, LANES), f32)], axis=0).T

    base = cls * (CSPLIT * cols) + me % CSPLIT * cols

    def hits(column, c):
        offset = column.astype(jnp.int32) - (base + c * width)
        return lax.broadcasted_iota(jnp.int32, (half, width), 1) == offset

    def chunk_body(c, carry):
        for r in range(PLANE):
            for m in range(1, PLANE):
                there = me + flip(r) + flip(m * PLANE)
                arrived(wcols.at[c, there], zrecv.at[(c * PLANE + r) * PLANE + m])

        def half_body(h, inner):
            logits = jnp.dot(
                feats[h].reshape(n_dp * half, depth), wcols[c].reshape(n_dp * depth_block, width),
                preferred_element_type=f32)
            held = jnp.zeros((half, LANES), f32)
            for i in range(n_dp):
                part = logits[i * half:(i + 1) * half]
                top = jnp.max(part, axis=1, keepdims=True)
                exponent = jnp.exp(part - top)
                exps[c, h, i] = exponent
                total = jnp.sum(exponent, axis=1, keepdims=True)
                square = jnp.sum(exponent * exponent, axis=1, keepdims=True)
                hit = hits(label_cols[h, :, i:i + 1], c)
                picked = jnp.sum(jnp.where(hit, part, 0.0), axis=1, keepdims=True)
                for s, value in enumerate((top, total, square, picked)):
                    held = jnp.where(lane == s * n_dp + i, value, held)
            marks[c, h] = held
            return inner

        return lax.fori_loop(0, 2, half_body, carry)

    lax.fori_loop(0, chunks, chunk_body, 0)

    pad = jnp.zeros((LANES - half, LANES), f32)
    for h in range(2):
        turned = [jnp.concatenate([marks[c, h], pad], axis=0).T for c in range(chunks)]
        part = [[t[s * n_dp:(s + 1) * n_dp] for t in turned] for s in range(4)]
        top = functools.reduce(jnp.maximum, part[0])
        fades = [jnp.exp(t - top) for t in part[0]]
        rows = (top,
                sum(t * f for t, f in zip(part[1], fades)),
                sum(t * f * f for t, f in zip(part[2], fades)),
                sum(part[3]))
        for c in range(chunks):
            maxima[c, h] = part[0][c]
        for s in range(4):
            for i in range(n_dp):
                stats[i, 4 * h + s:4 * h + s + 1, :] = rows[s][i:i + 1]

    for hop in range(1, count):
        there = (place + hop) % count
        sends.append(push(stats.at[there], all_stats.at[place], tsend.at[hop], trecv.at[hop], group_peer(hop)))
    all_stats[place] = stats[place]
    for hop in range(1, count):
        arrived(all_stats.at[(place + count - hop) % count], trecv.at[hop])

    for h in range(2):
        tops, totals, squares, picks = (all_stats[:, 4 * h + s, :] for s in range(4))
        row_max = jnp.max(tops, axis=0, keepdims=True)
        fade = jnp.exp(tops - row_max)
        row_total = jnp.sum(totals * fade, axis=0, keepdims=True)
        row_square = jnp.sum(squares * fade * fade, axis=0, keepdims=True)
        picked = jnp.sum(picks, axis=0, keepdims=True)
        spread = row_square / (row_total * row_total) - 2.0 * jnp.exp(picked - row_max) / row_total + 1.0
        energy = energy_rows[h:h + 1]
        factor = CLIP_NORM * lax.rsqrt(jnp.maximum(energy * spread, CLIP_NORM * CLIP_NORM))
        finals[4 * h:4 * h + 1, :] = row_max
        finals[4 * h + 1:4 * h + 2, :] = factor / row_total
        finals[4 * h + 2:4 * h + 3, :] = factor
        finals[4 * h + 3:4 * h + 4, :] = factor

    for hop in range(1, count):
        sends.append(push(finals, all_finals.at[place], gsend.at[hop], grecv.at[hop], group_peer(hop)))
    all_finals[place] = finals[...]
    for hop in range(1, count):
        arrived(all_finals.at[(place + count - hop) % count], grecv.at[hop])

    fill = jnp.zeros((LANES - 2 * n_dp, LANES), f32)
    for h in range(2):
        row_max, share, factor = (all_finals[:, 4 * h + s, :] for s in range(3))
        for c in range(chunks):
            scale = share * jnp.exp(maxima[c, h] - row_max)
            scale_cols[c, h] = jnp.concatenate([scale, factor, fill], axis=0).T[0:half]

    for copy in noise_copies:
        copy.wait()

    def out_copy(c):
        first = pl.multiple_of(c * width, width)
        return pltpu.make_async_copy(grads.at[c], out_ref.at[:, pl.ds(first, width)], out_sem.at[c])

    def grad_body(c, carry):
        for h in range(2):
            for i in range(n_dp):
                hit = hits(label_cols[h, :, i:i + 1], c)
                scale = scale_cols[c, h, :, i:i + 1]
                factor = scale_cols[c, h, :, n_dp + i:n_dp + i + 1]
                value = exps[c, h, i] * scale - jnp.where(hit, factor, 0.0)
                coefs[(h * n_dp + i) * half:(h * n_dp + i + 1) * half, :] = value.astype(coefs.dtype)
        grad = jnp.dot(turned_feats[...], coefs[...], preferred_element_type=f32)
        grads[c] = grad + NOISE_STD * grads[c]
        out_copy(c).start()
        return carry

    lax.fori_loop(0, chunks, grad_body, 0)
    for c in range(chunks):
        out_copy(c).wait()
    for c in (2, 3):
        sends.extend(column[c])
    for copy in sends:
        copy.wait_send()


def head(features, labels, weight, noise, n_dp, n_cls, row_block, col_block):
    rows, depth = features.shape
    half = rows // 2
    count = CSPLIT * n_cls
    width = col_block // CHUNKS
    anywhere = pl.BlockSpec(memory_space=pl.ANY)
    dma = pltpu.SemaphoreType.DMA
    f32 = jnp.float32
    bf16 = jnp.bfloat16
    return pl.pallas_call(
        functools.partial(head_kernel, n_dp, n_cls),
        out_shape=jax.ShapeDtypeStruct((row_block, col_block), f32),
        in_specs=[anywhere, pl.BlockSpec(memory_space=pltpu.VMEM), anywhere, anywhere],
        out_specs=anywhere,
        scratch_shapes=[
            pltpu.VMEM((2, n_dp, half, depth), bf16),
            pltpu.VMEM((row_block, n_dp * rows), bf16),
            pltpu.VMEM((CHUNKS, n_dp, weight.shape[0], width), bf16),
            pltpu.VMEM((CHUNKS, PLANE, weight.shape[0], width), bf16),
            pltpu.VMEM((CHUNKS, 2, n_dp, half, width), f32),
            pltpu.VMEM((CHUNKS, row_block, width), f32),
            pltpu.VMEM((n_dp * rows, width), bf16),
            pltpu.VMEM((n_dp, 1, 2 * LANES), jnp.int32),
            pltpu.VMEM((2, half, LANES), f32),
            pltpu.VMEM((CHUNKS, 2, half, LANES), f32),
            pltpu.VMEM((CHUNKS, 2, n_dp, LANES), f32),
            pltpu.VMEM((CHUNKS, 2, half, LANES), f32),
            pltpu.VMEM((count, 8, LANES), f32),
            pltpu.VMEM((count, 8, LANES), f32),
            pltpu.VMEM((8, LANES), f32),
            pltpu.VMEM((count, 8, LANES), f32),
            dma((n_dp * 4,)), dma((n_dp,)), dma((n_dp,)), dma((n_dp,)),
            dma((CHUNKS * 2 * PLANE,)), dma((CHUNKS * 2 * PLANE,)),
            dma((CHUNKS * PLANE * PLANE,)), dma((CHUNKS * PLANE * PLANE,)),
            dma((n_dp,)), dma((n_dp,)), dma((count,)), dma((count,)), dma((count,)), dma((count,)),
            dma((2 + CHUNKS,)), dma((CHUNKS,)), dma((CHUNKS,)),
        ],
        compiler_params=pltpu.CompilerParams(
            collective_id=0, has_side_effects=True, vmem_limit_bytes=60 << 20),
    )(features, labels, weight, noise)


def examples_split(features, labels, weight, noise):
    tok_rows = features.shape[0]
    feature_dim = features.shape[1]
    class_shard = weight.shape[1]
    groups = lax.axis_size("dp") // CSPLIT
    row_block = feature_dim // groups
    col_block = class_shard // CSPLIT
    slot_count = groups * CSPLIT
    feature_slots = jnp.broadcast_to(
        features.reshape(tok_rows, groups, 1, row_block), (tok_rows, groups, CSPLIT, row_block)
    ).reshape(tok_rows, slot_count, row_block)
    logits = jnp.dot(
        features,
        lax.all_gather(weight, "dp", axis=0, tiled=True),
        preferred_element_type=jnp.float32,
    )
    offset = labels - lax.axis_index("cls") * class_shard
    label_hit = lax.broadcasted_iota(jnp.int32, (tok_rows, class_shard), 1) == offset[:, None]
    onehot = label_hit.astype(jnp.float32)
    local_max = jnp.max(logits, axis=1)
    exponent = jnp.exp(logits - local_max[:, None])
    row_total = jnp.sum(exponent, axis=1)
    row_square = jnp.sum(exponent * exponent, axis=1)
    picked = jnp.sum(onehot * logits, axis=1)
    global_max = lax.pmax(local_max, "cls")
    rescale = jnp.exp(local_max - global_max)
    row_total, row_square, picked = lax.psum(
        (row_total * rescale, row_square * rescale * rescale, picked), "cls"
    )
    softmax = exponent * (jnp.exp(local_max - global_max) / row_total)[:, None]
    label_prob = jnp.exp(picked - global_max) / row_total
    spread = row_square / (row_total * row_total) - 2.0 * label_prob + 1.0
    energy = jnp.sum(jnp.square(features.astype(jnp.float32)), axis=1)
    factor = CLIP_NORM * lax.rsqrt(jnp.maximum(energy * spread, CLIP_NORM * CLIP_NORM))
    weighted = (factor[:, None] * (softmax - onehot)).astype(jnp.bfloat16)
    coef_slots = jnp.broadcast_to(
        weighted.reshape(tok_rows, 1, CSPLIT, col_block), (tok_rows, groups, CSPLIT, col_block)
    ).reshape(tok_rows, slot_count, col_block)
    feature_recv, coef_recv = (
        lax.all_to_all(feature_slots, "dp", split_axis=1, concat_axis=1, tiled=True),
        lax.all_to_all(coef_slots, "dp", split_axis=1, concat_axis=1, tiled=True),
    )
    grad_block = lax.dot_general(
        feature_recv, coef_recv, (((0, 1), (0, 1)), ((), ())), preferred_element_type=jnp.float32
    )
    return (grad_block + NOISE_STD * noise[0, 0]).reshape(noise.shape)


def on_device(features, labels, weight, noise):
    n_dp = lax.axis_size("dp")
    n_cls = lax.axis_size("cls")
    if n_dp != 2 * CSPLIT or n_cls != 2:
        return examples_split(features, labels, weight, noise)
    half = features.shape[0] // 2
    row_block = features.shape[1] // (n_dp // CSPLIT)
    col_block = weight.shape[1] // CSPLIT
    side = jnp.pad(labels.reshape(2, half), ((0, 0), (0, LANES - half))).reshape(1, 2 * LANES)
    grad = head(features, side, weight, noise[0, 0], n_dp, n_cls, row_block, col_block)
    return grad.reshape(noise.shape)


def solution(mesh):
    placed = (P("dp", None), P("dp"), P("dp", "cls"), P("dp", "cls", None, None))
    return jax.shard_map(
        on_device, mesh=mesh, in_specs=placed, out_specs=P("dp", "cls", None, None), check_vma=False
    )
```

```python
import functools

import jax
import jax.numpy as jnp
from jax import lax
from jax.experimental import pallas as pl
from jax.experimental.pallas import tpu as pltpu
from jax.sharding import PartitionSpec as P

CSPLIT = 8
CLIP_NORM = 40.0
NOISE_STD = 0.4
TILES = 4
PLANE = 4
LANES = 128
MESH = pl.DeviceIdType.MESH


def head_kernel(n_dp, n_cls, feat_ref, label_ref, weight_ref, noise_ref, out_ref,
                feats, turned_feats, wcols, wstage, exps, noise_buf, coefs, sides, label_cols, marks, maxima, early,
                stats, all_stats, finals, all_finals,
                fsend, frecv, bsend, brecv, psend, precv, zsend, zrecv, lsend, lrecv, tsend, trecv, gsend, grecv,
                local_sem, noise_sem):
    f32 = jnp.float32
    me = lax.axis_index("dp")
    cls = lax.axis_index("cls")
    sibling = 1 - cls
    stages = 4
    half, depth = feats.shape[2:]
    width = exps.shape[-1]
    cols = TILES * width
    last = TILES - 1
    row_block = turned_feats.shape[0]
    count = CSPLIT * n_cls
    place = me % CSPLIT * n_cls + cls
    level = me // PLANE
    spot = me % PLANE

    def group_peer(hop):
        there = (place + hop) % count
        return (me // CSPLIT * CSPLIT + there // n_cls, there % n_cls)

    barrier = pltpu.get_barrier_semaphore()
    for hop in range(1, n_dp):
        pl.semaphore_signal(barrier, inc=1, device_id=((me + hop) % n_dp, cls), device_id_type=MESH)
    for hop in range(1, count):
        pl.semaphore_signal(barrier, inc=1, device_id=group_peer(hop), device_id_type=MESH)
    pl.semaphore_wait(barrier, n_dp - 1 + count - 1)

    bit_step = [(1 << b) * (1 - 2 * ((me // (1 << b)) % 2)) for b in range(stages)]

    def flip(mask):
        return sum(bit_step[b] for b in range(stages) if mask >> b & 1)

    def stage_steps(which):
        return [bit_step[3], bit_step[2],
                bit_step[1] * (1 - which) + bit_step[0] * which,
                bit_step[0] * (1 - which) + bit_step[1] * which]

    steps = stage_steps(cls)
    sib_steps = stage_steps(sibling)

    def origin(mask, table):
        there = me
        for s in range(stages):
            if mask >> s & 1:
                there = there + table[s]
        return there

    sends = []

    def push(source, target, out_sem, in_sem, device):
        copy = pltpu.make_async_remote_copy(
            src_ref=source, dst_ref=target, send_sem=out_sem, recv_sem=in_sem,
            device_id=device, device_id_type=MESH,
        )
        copy.start()
        return copy

    def arrived(ref, sem):
        pltpu.make_async_remote_copy(
            src_ref=ref, dst_ref=ref, send_sem=sem, recv_sem=sem,
            device_id=(me, sibling), device_id_type=MESH,
        ).wait_recv()

    def left(ref, sem):
        pltpu.make_async_remote_copy(
            src_ref=ref, dst_ref=ref, send_sem=sem, recv_sem=sem,
            device_id=(me, sibling), device_id_type=MESH,
        ).wait_send()

    own_half = feat_ref.at[pl.ds(pl.multiple_of(cls * half, half), half)]

    def feat_forward(mask, first, last):
        source = feats.at[cls, origin(mask, steps)] if mask else own_half
        for s in range(max(mask.bit_length(), first), last):
            sends.append(push(source, feats.at[cls, origin(mask, steps)], fsend.at[mask * stages + s],
                              frecv.at[mask | 1 << s], (me + steps[s], cls)))

    def feat_share(mask):
        block = feats.at[cls, origin(mask, steps)]
        sends.append(push(block, block, bsend.at[mask], brecv.at[mask], (me, sibling)))

    def feat_step(mask):
        arrived(feats.at[cls, origin(mask, steps)], frecv.at[mask])
        feat_forward(mask, 0, stages)
        feat_share(mask)

    parity = level % 2

    def block_cols(side, there, c):
        return pl.ds(pl.multiple_of((side * PLANE + there) * cols + c * width, LANES), width)

    def plane_send(c):
        for r in range(1, PLANE):
            peer = me + flip(r)
            at = c * 2 * PLANE + r * 2
            sends.append(push(weight_ref.at[:, block_cols(parity, peer % PLANE, c)], wcols.at[c, me],
                              psend.at[at], precv.at[at], (peer, cls)))
            sends.append(push(weight_ref.at[:, block_cols(1 - parity, peer % PLANE, c)], wstage.at[c, spot],
                              psend.at[at + 1], precv.at[at + 1], (peer, cls)))

    def plane_of(where):
        return pl.ds(pl.multiple_of(where * PLANE, PLANE), PLANE)

    def column_send(c):
        for r in range(1, PLANE):
            at = c * 2 * PLANE + r * 2
            arrived(wcols.at[c, me + flip(r)], precv.at[at])
            arrived(wstage.at[c, (me + flip(r)) % PLANE], precv.at[at + 1])
        for copy in keep[c]:
            copy.wait()
        block = wcols.at[c, plane_of(level)]
        for m in (2, 3, 1):
            at = c * PLANE + m
            push(block if m == 2 else wstage.at[c], block, zsend.at[at], zrecv.at[at], (me + flip(m * PLANE), cls))

    def sent(c):
        for m in range(1, PLANE):
            left(wstage.at[c], zsend.at[c * PLANE + m])

    feat_forward(0, 0, 2)
    plane_send(0)
    plane_send(1)
    keep = [[pltpu.make_async_copy(weight_ref.at[:, block_cols(parity, spot, c)], wcols.at[c, me],
                                   local_sem.at[2 * c]),
             pltpu.make_async_copy(weight_ref.at[:, block_cols(1 - parity, spot, c)], wstage.at[c, spot],
                                   local_sem.at[2 * c + 1])] for c in range(TILES)]
    own_feats = [pltpu.make_async_copy(feat_ref.at[pl.ds(h * half, half)], feats.at[h, me],
                                       local_sem.at[2 * TILES + h]) for h in range(2)]
    for copy in sum(keep, own_feats):
        copy.start()
    noise_copy = pltpu.make_async_copy(noise_ref, noise_buf, noise_sem)
    sides[me, :, 0:2 * half] = label_ref[...]
    for hop in range(1, n_dp):
        sends.append(push(sides.at[me], sides.at[me], lsend.at[hop], lrecv.at[hop], ((me + hop) % n_dp, cls)))

    feat_forward(0, 2, stages)
    column_send(0)
    for mask in (4, 8, 12):
        feat_step(mask)
    column_send(1)
    plane_send(2)
    for mask in (2, 6, 10, 14, 1, 5, 9, 13):
        feat_step(mask)
    noise_copy.start()
    sent(0)
    column_send(2)
    plane_send(3)
    for mask in (3, 7, 11, 15):
        feat_step(mask)
    sent(1)
    column_send(3)
    for mask in range(1, 16):
        arrived(feats.at[sibling, origin(mask, sib_steps)], brecv.at[mask])

    for hop in range(1, n_dp):
        arrived(sides.at[(me + n_dp - hop) % n_dp], lrecv.at[hop])
    for copy in own_feats:
        copy.wait()

    rows = jnp.concatenate([sides[i] for i in range(n_dp)], axis=0).astype(f32)
    rows = jnp.concatenate([rows, jnp.zeros((LANES - n_dp, 2 * LANES), f32)], axis=0).T
    for h in range(2):
        label_cols[h] = rows[h * half:(h + 1) * half]

    first_row = pl.multiple_of(me // CSPLIT * row_block, row_block)
    quad = LANES // 32

    def turn_body(t, carry):
        h, k = t // (n_dp // quad), t % (n_dp // quad)
        part = feats[h, pl.ds(k * quad, quad), :, pl.ds(first_row, row_block)].reshape(quad * half, row_block)
        turned_feats[:, pl.ds(pl.multiple_of(t * quad * half, LANES), quad * half)] = part.T
        return carry

    lax.fori_loop(0, 2 * n_dp // quad, turn_body, 0)

    lane = lax.broadcasted_iota(jnp.int32, (half, LANES), 1)
    energy_cols = jnp.zeros((half, LANES), f32)
    for h in range(2):
        value = feats[h, place].astype(f32)
        energy_cols = jnp.where(lane == h, jnp.sum(value * value, axis=1, keepdims=True), energy_cols)
    energy_rows = jnp.concatenate([energy_cols, jnp.zeros((LANES - half, LANES), f32)], axis=0).T

    base = cls * (CSPLIT * cols) + me % CSPLIT * cols

    def hits(labels, c):
        offset = labels.astype(jnp.int32) - (base + c * width)
        return lax.broadcasted_iota(jnp.int32, (half, width), 1) == offset

    def measure(logits, c, h):
        held = jnp.zeros((half, LANES), f32)
        for i in range(n_dp):
            part = logits[i * half:(i + 1) * half]
            top = jnp.max(part, axis=1, keepdims=True)
            exponent = jnp.exp(part - top)
            exps[c, h, i] = exponent
            total = jnp.sum(exponent, axis=1, keepdims=True)
            square = jnp.sum(exponent * exponent, axis=1, keepdims=True)
            hit = hits(label_cols[h, :, i:i + 1], c)
            picked = jnp.sum(jnp.where(hit, exponent, 0.0), axis=1, keepdims=True)
            for s, value in enumerate((top, total, square, picked)):
                held = jnp.where(lane == s * n_dp + i, value, held)
        marks[c, h] = held

    def take(block, c, m):
        arrived(block.at[plane_of((me + flip(m * PLANE)) // PLANE)], zrecv.at[c * PLANE + m])

    def whole_dot(h, block):
        return jnp.dot(feats[h].reshape(n_dp * half, depth), block[...].reshape(depth, block.shape[-1]),
                       preferred_element_type=f32)

    def chunk_body(c, carry):
        block = wcols.at[c]

        for m in range(1, PLANE):
            take(block, c, m)

        def half_body(h, inner):
            measure(whole_dot(h, block), c, h)
            return inner

        return lax.fori_loop(0, 2, half_body, carry)

    lax.fori_loop(0, TILES - 1, chunk_body, 0)

    pad = jnp.zeros((LANES - half, LANES), f32)

    def turned_marks(c, h):
        turned = jnp.concatenate([marks[c, h], pad], axis=0).T
        maxima[c, h] = turned[0:n_dp]
        return [turned[s * n_dp:(s + 1) * n_dp] for s in range(4)]

    def merged(parts):
        top = functools.reduce(jnp.maximum, [part[0] for part in parts])
        fades = [jnp.exp(part[0] - top) for part in parts]
        return [top] + [sum(part[s] * (f * f if s == 2 else f) for part, f in zip(parts, fades)) for s in range(1, 4)]

    side = me // CSPLIT

    def part_dot(h, which):
        first = pl.multiple_of(which * row_block, row_block)
        return jnp.dot(
            feats[h, :, :, pl.ds(first, row_block)].reshape(n_dp * half, row_block),
            wcols[last, pl.ds(which * CSPLIT, CSPLIT)].reshape(row_block, width),
            preferred_element_type=f32)

    take(wcols.at[last], last, 1)

    def near_body(h, carry):
        exps[last, h] = part_dot(h, side).reshape(n_dp, half, width)
        return carry

    lax.fori_loop(0, 2, near_body, 0)
    sent(last - 1)
    for copy in sends:
        copy.wait_send()
    for h in range(2):
        for s, row in enumerate(merged([turned_marks(c, h) for c in range(last)])):
            early[h, s] = row
    take(wcols.at[last], last, 2)
    take(wcols.at[last], last, 3)

    def join(h):
        rows = merged([[early[h, s] for s in range(4)], turned_marks(last, h)])
        for s in range(4):
            for i in range(n_dp):
                stats[h, i, s:s + 1, :] = rows[s][i:i + 1]
        for hop in range(1, count):
            there = (place + hop) % count
            push(stats.at[h, there], all_stats.at[h, place], tsend.at[h * count + hop],
                 trecv.at[h * count + hop], group_peer(hop))
        all_stats[h, place] = stats[h, place]

    def settle(h):
        for hop in range(1, count):
            arrived(all_stats.at[h, (place + count - hop) % count], trecv.at[h * count + hop])
        tops, totals, squares, picks = (all_stats[h, :, s, :] for s in range(4))
        row_max = jnp.max(tops, axis=0, keepdims=True)
        fade = jnp.exp(tops - row_max)
        row_total = jnp.sum(totals * fade, axis=0, keepdims=True)
        row_square = jnp.sum(squares * fade * fade, axis=0, keepdims=True)
        picked = jnp.sum(picks * fade, axis=0, keepdims=True)
        spread = row_square / (row_total * row_total) - 2.0 * picked / row_total + 1.0
        energy = energy_rows[h:h + 1]
        factor = CLIP_NORM * lax.rsqrt(jnp.maximum(energy * spread, CLIP_NORM * CLIP_NORM))
        finals[h, 0:1, :] = row_max
        finals[h, 1:2, :] = factor / row_total
        finals[h, 2:3, :] = factor
        finals[h, 3:4, :] = factor
        for hop in range(1, count):
            push(finals.at[h], all_finals.at[h, place], gsend.at[h * count + hop],
                 grecv.at[h * count + hop], group_peer(hop))
        all_finals[h, place] = finals[h]

    fill = jnp.zeros((LANES - (TILES + 1) * n_dp, LANES), f32)

    def scales(h):
        for hop in range(1, count):
            arrived(all_finals.at[h, (place + count - hop) % count], grecv.at[h * count + hop])
        row_max, share, factor = (all_finals[h, :, s, :] for s in range(3))
        scale = [share * jnp.exp(maxima[c, h] - row_max) for c in range(TILES)]
        marks[0, h] = jnp.concatenate(scale + [factor, fill], axis=0).T[0:half]

    def coefficients(h, c):
        for i in range(n_dp):
            hit = hits(label_cols[h, :, i:i + 1], c)
            scale = marks[0, h, :, c * n_dp + i:c * n_dp + i + 1]
            factor = marks[0, h, :, last * n_dp + n_dp + i:last * n_dp + n_dp + i + 1]
            value = exps[c, h, i] * scale - jnp.where(hit, factor, 0.0)
            coefs[c % 2, i * half:(i + 1) * half, :] = value.astype(coefs.dtype)

    def far_body(h, carry):
        measure(exps[last, h].reshape(n_dp * half, width) + part_dot(h, 1 - side), last, h)
        join(h)
        return carry

    lax.fori_loop(0, 2, far_body, 0)
    settle(0)
    settle(1)
    noise_copy.wait()
    scales(0)
    coefficients(0, 0)
    for h in range(2):
        for c in range(TILES):
            if c + 1 < TILES:
                coefficients(h, c + 1)
            elif h == 0:
                scales(1)
                coefficients(1, 0)
            at = slice(c * width, (c + 1) * width)
            begin = h * n_dp * half
            grad = jnp.dot(turned_feats[:, begin:begin + n_dp * half], coefs[c % 2], preferred_element_type=f32)
            out_ref[:, at] = grad + (out_ref[:, at] if h else NOISE_STD * noise_buf[:, at])
    sent(last)
    for h in range(2):
        for hop in range(1, count):
            left(stats.at[h, 0], tsend.at[h * count + hop])
            left(finals.at[h], gsend.at[h * count + hop])


def head(features, labels, weight, noise, n_dp, n_cls, row_block, col_block):
    rows, depth = features.shape
    half = rows // 2
    count = CSPLIT * n_cls
    width = col_block // TILES
    depth_block = weight.shape[0]
    anywhere = pl.BlockSpec(memory_space=pl.ANY)
    dma = pltpu.SemaphoreType.DMA
    f32 = jnp.float32
    bf16 = jnp.bfloat16
    return pl.pallas_call(
        functools.partial(head_kernel, n_dp, n_cls),
        out_shape=pltpu.VMEM((row_block, col_block), f32),
        in_specs=[anywhere, pl.BlockSpec(memory_space=pltpu.VMEM), anywhere, anywhere],
        out_specs=pl.BlockSpec(memory_space=pltpu.VMEM),
        scratch_shapes=[
            pltpu.VMEM((2, n_dp, half, depth), bf16),
            pltpu.VMEM((row_block, n_dp * rows), bf16),
            pltpu.VMEM((TILES, n_dp, depth_block, width), bf16),
            pltpu.VMEM((TILES, PLANE, depth_block, width), bf16),
            pltpu.VMEM((TILES, 2, n_dp, half, width), f32),
            pltpu.VMEM((row_block, col_block), f32),
            pltpu.VMEM((2, n_dp * half, width), bf16),
            pltpu.VMEM((n_dp, 1, 2 * LANES), jnp.int32),
            pltpu.VMEM((2, half, LANES), f32),
            pltpu.VMEM((TILES, 2, half, LANES), f32),
            pltpu.VMEM((TILES, 2, n_dp, LANES), f32),
            pltpu.VMEM((2, 4, n_dp, LANES), f32),
            pltpu.VMEM((2, count, 4, LANES), f32),
            pltpu.VMEM((2, count, 4, LANES), f32),
            pltpu.VMEM((2, 4, LANES), f32),
            pltpu.VMEM((2, count, 4, LANES), f32),
            dma((n_dp * 4,)), dma((n_dp,)), dma((n_dp,)), dma((n_dp,)),
            dma((TILES * 2 * PLANE,)), dma((TILES * 2 * PLANE,)),
            dma((TILES * PLANE,)), dma((TILES * PLANE,)),
            dma((n_dp,)), dma((n_dp,)), dma((2 * count,)), dma((2 * count,)), dma((2 * count,)), dma((2 * count,)),
            dma((2 * TILES + 2,)), dma,
        ],
        compiler_params=pltpu.CompilerParams(
            collective_id=0, has_side_effects=True, vmem_limit_bytes=55 << 20),
    )(features, labels, weight, noise)


def examples_split(features, labels, weight, noise):
    tok_rows = features.shape[0]
    feature_dim = features.shape[1]
    class_shard = weight.shape[1]
    groups = lax.axis_size("dp") // CSPLIT
    row_block = feature_dim // groups
    col_block = class_shard // CSPLIT
    slot_count = groups * CSPLIT
    feature_slots = jnp.broadcast_to(
        features.reshape(tok_rows, groups, 1, row_block), (tok_rows, groups, CSPLIT, row_block)
    ).reshape(tok_rows, slot_count, row_block)
    logits = jnp.dot(
        features,
        lax.all_gather(weight, "dp", axis=0, tiled=True),
        preferred_element_type=jnp.float32,
    )
    offset = labels - lax.axis_index("cls") * class_shard
    label_hit = lax.broadcasted_iota(jnp.int32, (tok_rows, class_shard), 1) == offset[:, None]
    onehot = label_hit.astype(jnp.float32)
    local_max = jnp.max(logits, axis=1)
    exponent = jnp.exp(logits - local_max[:, None])
    row_total = jnp.sum(exponent, axis=1)
    row_square = jnp.sum(exponent * exponent, axis=1)
    picked = jnp.sum(onehot * logits, axis=1)
    global_max = lax.pmax(local_max, "cls")
    rescale = jnp.exp(local_max - global_max)
    row_total, row_square, picked = lax.psum(
        (row_total * rescale, row_square * rescale * rescale, picked), "cls"
    )
    softmax = exponent * (jnp.exp(local_max - global_max) / row_total)[:, None]
    label_prob = jnp.exp(picked - global_max) / row_total
    spread = row_square / (row_total * row_total) - 2.0 * label_prob + 1.0
    energy = jnp.sum(jnp.square(features.astype(jnp.float32)), axis=1)
    factor = CLIP_NORM * lax.rsqrt(jnp.maximum(energy * spread, CLIP_NORM * CLIP_NORM))
    weighted = (factor[:, None] * (softmax - onehot)).astype(jnp.bfloat16)
    coef_slots = jnp.broadcast_to(
        weighted.reshape(tok_rows, 1, CSPLIT, col_block), (tok_rows, groups, CSPLIT, col_block)
    ).reshape(tok_rows, slot_count, col_block)
    feature_recv, coef_recv = (
        lax.all_to_all(feature_slots, "dp", split_axis=1, concat_axis=1, tiled=True),
        lax.all_to_all(coef_slots, "dp", split_axis=1, concat_axis=1, tiled=True),
    )
    grad_block = lax.dot_general(
        feature_recv, coef_recv, (((0, 1), (0, 1)), ((), ())), preferred_element_type=jnp.float32
    )
    return (grad_block + NOISE_STD * noise[0, 0]).reshape(noise.shape)


def on_device(features, labels, weight, noise):
    n_dp = lax.axis_size("dp")
    n_cls = lax.axis_size("cls")
    if n_dp != 2 * CSPLIT or n_cls != 2:
        return examples_split(features, labels, weight, noise)
    half = features.shape[0] // 2
    row_block = features.shape[1] // (n_dp // CSPLIT)
    col_block = weight.shape[1] // CSPLIT
    grad = head(features, labels.reshape(1, 2 * half), weight, noise[0, 0], n_dp, n_cls, row_block, col_block)
    return grad.reshape(noise.shape)


def solution(mesh):
    placed = (P("dp", None), P("dp"), P("dp", "cls"), P("dp", "cls", None, None))
    return jax.shard_map(
        on_device, mesh=mesh, in_specs=placed, out_specs=P("dp", "cls", None, None), check_vma=False
    )
```

```python
import functools

import jax
import jax.numpy as jnp
from jax import lax
from jax.experimental import pallas as pl
from jax.experimental.pallas import tpu as pltpu
from jax.sharding import PartitionSpec as P

CSPLIT = 8
CLIP_NORM = 40.0
NOISE_STD = 0.4
TILES = 4
PARTS = 2
PLANE = 4
LANES = 128
MESH = pl.DeviceIdType.MESH


def head_kernel(n_dp, n_cls, feat_ref, label_ref, weight_ref, noise_ref, out_ref,
                feats, turned_feats, wcols, wstage, exps, noise_buf, coefs, sides, label_cols, marks, maxima, early,
                stats, all_stats, finals, all_finals,
                fsend, frecv, bsend, brecv, psend, precv, zsend, zrecv, lsend, lrecv, tsend, trecv, gsend, grecv,
                local_sem, noise_sem):
    f32 = jnp.float32
    me = lax.axis_index("dp")
    cls = lax.axis_index("cls")
    sibling = 1 - cls
    stages = 4
    half, depth = feats.shape[2:]
    width = exps.shape[-1]
    cols = TILES * width
    last = TILES - 1
    row_block = turned_feats.shape[0]
    count = CSPLIT * n_cls
    place = me % CSPLIT * n_cls + cls
    level = me // PLANE
    spot = me % PLANE

    bit_step = [(1 << b) * (1 - 2 * ((me // (1 << b)) % 2)) for b in range(stages)]

    def flip(mask):
        return sum(bit_step[b] for b in range(stages) if mask >> b & 1)

    hops = sorted(range(1, count), key=lambda hop: (-(hop >> 1).bit_count(), hop))
    core_step = 1 - 2 * cls

    def group_peer(hop):
        return (me + flip(hop >> 1), cls + (hop & 1) * core_step)

    def peer_place(hop):
        return place + flip(hop >> 1) * n_cls + (hop & 1) * core_step

    barrier = pltpu.get_barrier_semaphore()
    crossed = [hop for hop in hops if hop & 1]
    for mask in sorted(range(1, n_dp), key=lambda mask: -((mask >> 2) + (mask & 3).bit_count())):
        pl.semaphore_signal(barrier, inc=1, device_id=(me + flip(mask), cls), device_id_type=MESH)
    for hop in crossed:
        pl.semaphore_signal(barrier, inc=1, device_id=group_peer(hop), device_id_type=MESH)
    pl.semaphore_wait(barrier, n_dp - 1 + len(crossed))

    def stage_steps(which):
        return [bit_step[3], bit_step[2],
                bit_step[1] * (1 - which) + bit_step[0] * which,
                bit_step[0] * (1 - which) + bit_step[1] * which]

    steps = stage_steps(cls)
    sib_steps = stage_steps(sibling)

    def origin(mask, table):
        there = me
        for s in range(stages):
            if mask >> s & 1:
                there = there + table[s]
        return there

    sends = []

    def push(source, target, out_sem, in_sem, device):
        copy = pltpu.make_async_remote_copy(
            src_ref=source, dst_ref=target, send_sem=out_sem, recv_sem=in_sem,
            device_id=device, device_id_type=MESH,
        )
        copy.start()
        return copy

    def arrived(ref, sem):
        pltpu.make_async_remote_copy(
            src_ref=ref, dst_ref=ref, send_sem=sem, recv_sem=sem,
            device_id=(me, sibling), device_id_type=MESH,
        ).wait_recv()

    def left(ref, sem):
        pltpu.make_async_remote_copy(
            src_ref=ref, dst_ref=ref, send_sem=sem, recv_sem=sem,
            device_id=(me, sibling), device_id_type=MESH,
        ).wait_send()

    own_half = feat_ref.at[pl.ds(pl.multiple_of(cls * half, half), half)]

    def feat_forward(mask, first, last):
        source = feats.at[cls, origin(mask, steps)] if mask else own_half
        for s in range(max(mask.bit_length(), first), last):
            sends.append(push(source, feats.at[cls, origin(mask, steps)], fsend.at[mask * stages + s],
                              frecv.at[mask | 1 << s], (me + steps[s], cls)))

    def feat_share(mask):
        block = feats.at[cls, origin(mask, steps)]
        sends.append(push(block, block, bsend.at[mask], brecv.at[mask], (me, sibling)))

    def feat_step(mask):
        arrived(feats.at[cls, origin(mask, steps)], frecv.at[mask])
        feat_forward(mask, 0, stages)
        feat_share(mask)

    parity = level % 2

    def block_cols(side, there, c):
        return pl.ds(pl.multiple_of((side * PLANE + there) * cols + c * width, LANES), width)

    def plane_send(c):
        for r in range(1, PLANE):
            peer = me + flip(r)
            at = c * 2 * PLANE + r * 2
            sends.append(push(weight_ref.at[:, block_cols(parity, peer % PLANE, c)], wcols.at[c, me],
                              psend.at[at], precv.at[at], (peer, cls)))
            sends.append(push(weight_ref.at[:, block_cols(1 - parity, peer % PLANE, c)], wstage.at[c, spot],
                              psend.at[at + 1], precv.at[at + 1], (peer, cls)))

    def plane_of(where):
        return pl.ds(pl.multiple_of(where * PLANE, PLANE), PLANE)

    def column_send(c):
        for r in range(1, PLANE):
            at = c * 2 * PLANE + r * 2
            arrived(wcols.at[c, me + flip(r)], precv.at[at])
            arrived(wstage.at[c, (me + flip(r)) % PLANE], precv.at[at + 1])
        for copy in keep[c]:
            copy.wait()
        block = wcols.at[c, plane_of(level)]
        for m in (2, 3, 1):
            at = c * PLANE + m
            push(block if m == 2 else wstage.at[c], block, zsend.at[at], zrecv.at[at], (me + flip(m * PLANE), cls))

    def sent(c):
        for m in range(1, PLANE):
            left(wstage.at[c], zsend.at[c * PLANE + m])

    feat_forward(0, 0, 2)
    plane_send(0)
    plane_send(1)
    keep = [[pltpu.make_async_copy(weight_ref.at[:, block_cols(parity, spot, c)], wcols.at[c, me],
                                   local_sem.at[2 * c]),
             pltpu.make_async_copy(weight_ref.at[:, block_cols(1 - parity, spot, c)], wstage.at[c, spot],
                                   local_sem.at[2 * c + 1])] for c in range(TILES)]
    own_feats = [pltpu.make_async_copy(feat_ref.at[pl.ds(h * half, half)], feats.at[h, me],
                                       local_sem.at[2 * TILES + h]) for h in range(2)]
    for copy in sum(keep, own_feats):
        copy.start()
    noise_copy = pltpu.make_async_copy(noise_ref, noise_buf, noise_sem)
    sides[me, :, 0:2 * half] = label_ref[...]
    for hop in range(1, n_dp):
        sends.append(push(sides.at[me], sides.at[me], lsend.at[hop], lrecv.at[hop], (me + flip(hop), cls)))

    feat_forward(0, 2, stages)
    column_send(0)
    for mask in (4, 8, 12):
        feat_step(mask)
    column_send(1)
    plane_send(2)
    for mask in (2, 6, 10, 14, 1, 5, 9, 13):
        feat_step(mask)
    noise_copy.start()
    sent(0)
    column_send(2)
    plane_send(3)
    for mask in (3, 7, 11, 15):
        feat_step(mask)
    sent(1)
    column_send(3)
    for mask in range(1, 16):
        arrived(feats.at[sibling, origin(mask, sib_steps)], brecv.at[mask])

    for hop in range(1, n_dp):
        arrived(sides.at[me + flip(hop)], lrecv.at[hop])
    for copy in own_feats:
        copy.wait()

    rows = jnp.concatenate([sides[i] for i in range(n_dp)], axis=0).astype(f32)
    rows = jnp.concatenate([rows, jnp.zeros((LANES - n_dp, 2 * LANES), f32)], axis=0).T
    for h in range(2):
        label_cols[h] = rows[h * half:(h + 1) * half]

    first_row = pl.multiple_of(me // CSPLIT * row_block, row_block)
    quad = LANES // 32

    def turn_body(t, carry):
        h, k = t // (n_dp // quad), t % (n_dp // quad)
        part = feats[h, pl.ds(k * quad, quad), :, pl.ds(first_row, row_block)].reshape(quad * half, row_block)
        turned_feats[:, pl.ds(pl.multiple_of(t * quad * half, LANES), quad * half)] = part.T
        return carry

    lax.fori_loop(0, 2 * n_dp // quad, turn_body, 0)

    lane = lax.broadcasted_iota(jnp.int32, (half, LANES), 1)
    energy_cols = jnp.zeros((half, LANES), f32)
    for h in range(2):
        value = feats[h, place].astype(f32)
        energy_cols = jnp.where(lane == h, jnp.sum(value * value, axis=1, keepdims=True), energy_cols)
    energy_rows = jnp.concatenate([energy_cols, jnp.zeros((LANES - half, LANES), f32)], axis=0).T

    base = cls * (CSPLIT * cols) + me % CSPLIT * cols

    def hits(labels, c):
        offset = labels.astype(jnp.int32) - (base + c * width)
        return lax.broadcasted_iota(jnp.int32, (half, width), 1) == offset

    def observe(logits, c, h, blocks, held):
        for k, i in enumerate(blocks):
            part = logits[k * half:(k + 1) * half]
            top = jnp.max(part, axis=1, keepdims=True)
            exponent = jnp.exp(part - top)
            exps[c, h, i] = exponent
            total = jnp.sum(exponent, axis=1, keepdims=True)
            square = jnp.sum(exponent * exponent, axis=1, keepdims=True)
            hit = hits(label_cols[h, :, i:i + 1], c)
            picked = jnp.sum(jnp.where(hit, exponent, 0.0), axis=1, keepdims=True)
            for s, value in enumerate((top, total, square, picked)):
                held = jnp.where(lane == s * n_dp + i, value, held)
        return held

    def measure(logits, c, h):
        marks[c, h] = observe(logits, c, h, range(n_dp), jnp.zeros((half, LANES), f32))

    def take(block, c, m):
        arrived(block.at[plane_of((me + flip(m * PLANE)) // PLANE)], zrecv.at[c * PLANE + m])

    def whole_dot(h, block):
        return jnp.dot(feats[h].reshape(n_dp * half, depth), block[...].reshape(depth, block.shape[-1]),
                       preferred_element_type=f32)

    def chunk_body(c, carry):
        block = wcols.at[c]

        for m in range(1, PLANE):
            take(block, c, m)

        def half_body(h, inner):
            measure(whole_dot(h, block), c, h)
            return inner

        return lax.fori_loop(0, 2, half_body, carry)

    lax.fori_loop(0, TILES - 1, chunk_body, 0)

    pad = jnp.zeros((LANES - half, LANES), f32)

    def turned_marks(c, h):
        turned = jnp.concatenate([marks[c, h], pad], axis=0).T
        maxima[c, h] = turned[0:n_dp]
        return [turned[s * n_dp:(s + 1) * n_dp] for s in range(4)]

    def merged(parts):
        top = functools.reduce(jnp.maximum, [part[0] for part in parts])
        fades = [jnp.exp(part[0] - top) for part in parts]
        return [top] + [sum(part[s] * (f * f if s == 2 else f) for part, f in zip(parts, fades)) for s in range(1, 4)]

    side = me // CSPLIT

    team = n_dp // PARTS

    def part_dot(h, g, which):
        first = pl.multiple_of(which * row_block, row_block)
        return jnp.dot(
            feats[h, pl.ds(g * team, team), :, pl.ds(first, row_block)].reshape(team * half, row_block),
            wcols[last, pl.ds(which * CSPLIT, CSPLIT)].reshape(row_block, width),
            preferred_element_type=f32)

    take(wcols.at[last], last, 1)

    def near_body(k, carry):
        out_ref[0:team * half, pl.ds(pl.multiple_of(k * width, width), width)] = part_dot(k // PARTS, k % PARTS, side)
        return carry

    lax.fori_loop(0, 2 * PARTS, near_body, 0)
    sent(last - 1)
    for copy in sends:
        copy.wait_send()
    for h in range(2):
        for s, row in enumerate(merged([turned_marks(c, h) for c in range(last)])):
            early[h, s] = row
    take(wcols.at[last], last, 2)
    take(wcols.at[last], last, 3)

    def join(h):
        rows = merged([[early[h, s] for s in range(4)], turned_marks(last, h)])
        for s in range(4):
            for i in range(n_dp):
                stats[h, i, s:s + 1, :] = rows[s][i:i + 1]
        for hop in hops:
            push(stats.at[h, peer_place(hop)], all_stats.at[h, place], tsend.at[h * count + hop],
                 trecv.at[h * count + hop], group_peer(hop))
        all_stats[h, place] = stats[h, place]

    def settle(h):
        for hop in hops:
            arrived(all_stats.at[h, peer_place(hop)], trecv.at[h * count + hop])
        tops, totals, squares, picks = (all_stats[h, :, s, :] for s in range(4))
        row_max = jnp.max(tops, axis=0, keepdims=True)
        fade = jnp.exp(tops - row_max)
        row_total = jnp.sum(totals * fade, axis=0, keepdims=True)
        row_square = jnp.sum(squares * fade * fade, axis=0, keepdims=True)
        picked = jnp.sum(picks * fade, axis=0, keepdims=True)
        spread = row_square / (row_total * row_total) - 2.0 * picked / row_total + 1.0
        energy = energy_rows[h:h + 1]
        factor = CLIP_NORM * lax.rsqrt(jnp.maximum(energy * spread, CLIP_NORM * CLIP_NORM))
        finals[h, 0:1, :] = row_max
        finals[h, 1:2, :] = factor / row_total
        finals[h, 2:3, :] = factor
        finals[h, 3:4, :] = factor
        for hop in hops:
            push(finals.at[h], all_finals.at[h, place], gsend.at[h * count + hop],
                 grecv.at[h * count + hop], group_peer(hop))
        all_finals[h, place] = finals[h]

    fill = jnp.zeros((LANES - (TILES + 1) * n_dp, LANES), f32)

    def scales(h):
        for hop in hops:
            arrived(all_finals.at[h, peer_place(hop)], grecv.at[h * count + hop])
        row_max, share, factor = (all_finals[h, :, s, :] for s in range(3))
        scale = [share * jnp.exp(maxima[c, h] - row_max) for c in range(TILES)]
        marks[0, h] = jnp.concatenate(scale + [factor, fill], axis=0).T[0:half]

    def coefficients(h, c):
        for i in range(n_dp):
            hit = hits(label_cols[h, :, i:i + 1], c)
            scale = marks[0, h, :, c * n_dp + i:c * n_dp + i + 1]
            factor = marks[0, h, :, last * n_dp + n_dp + i:last * n_dp + n_dp + i + 1]
            value = exps[c, h, i] * scale - jnp.where(hit, factor, 0.0)
            coefs[c % 2, i * half:(i + 1) * half, :] = value.astype(coefs.dtype)

    def far_body(h, carry):
        logits = [
            out_ref[0:team * half, pl.ds(pl.multiple_of((h * PARTS + g) * width, width), width)]
            + part_dot(h, g, 1 - side) for g in range(PARTS)]
        held = jnp.zeros((half, LANES), f32)
        for g in range(PARTS):
            held = observe(logits[g], last, h, range(g * team, (g + 1) * team), held)
        marks[last, h] = held
        join(h)
        return carry

    lax.fori_loop(0, 2, far_body, 0)
    settle(0)
    settle(1)
    noise_copy.wait()
    scales(0)
    coefficients(0, 0)
    for h in range(2):
        for c in range(TILES):
            if c + 1 < TILES:
                coefficients(h, c + 1)
            elif h == 0:
                scales(1)
                coefficients(1, 0)
            at = slice(c * width, (c + 1) * width)
            begin = h * n_dp * half
            grad = jnp.dot(turned_feats[:, begin:begin + n_dp * half], coefs[c % 2], preferred_element_type=f32)
            out_ref[:, at] = grad + (out_ref[:, at] if h else NOISE_STD * noise_buf[:, at])
    sent(last)
    for h in range(2):
        for hop in range(1, count):
            left(stats.at[h, 0], tsend.at[h * count + hop])
            left(finals.at[h], gsend.at[h * count + hop])


def head(features, labels, weight, noise, n_dp, n_cls, row_block, col_block):
    rows, depth = features.shape
    half = rows // 2
    count = CSPLIT * n_cls
    width = col_block // TILES
    depth_block = weight.shape[0]
    anywhere = pl.BlockSpec(memory_space=pl.ANY)
    dma = pltpu.SemaphoreType.DMA
    f32 = jnp.float32
    bf16 = jnp.bfloat16
    return pl.pallas_call(
        functools.partial(head_kernel, n_dp, n_cls),
        out_shape=pltpu.VMEM((row_block, col_block), f32),
        in_specs=[anywhere, pl.BlockSpec(memory_space=pltpu.VMEM), anywhere, anywhere],
        out_specs=pl.BlockSpec(memory_space=pltpu.VMEM),
        scratch_shapes=[
            pltpu.VMEM((2, n_dp, half, depth), bf16),
            pltpu.VMEM((row_block, n_dp * rows), bf16),
            pltpu.VMEM((TILES, n_dp, depth_block, width), bf16),
            pltpu.VMEM((TILES, PLANE, depth_block, width), bf16),
            pltpu.VMEM((TILES, 2, n_dp, half, width), f32),
            pltpu.VMEM((row_block, col_block), f32),
            pltpu.VMEM((2, n_dp * half, width), bf16),
            pltpu.VMEM((n_dp, 1, 2 * LANES), jnp.int32),
            pltpu.VMEM((2, half, LANES), f32),
            pltpu.VMEM((TILES, 2, half, LANES), f32),
            pltpu.VMEM((TILES, 2, n_dp, LANES), f32),
            pltpu.VMEM((2, 4, n_dp, LANES), f32),
            pltpu.VMEM((2, count, 4, LANES), f32),
            pltpu.VMEM((2, count, 4, LANES), f32),
            pltpu.VMEM((2, 4, LANES), f32),
            pltpu.VMEM((2, count, 4, LANES), f32),
            dma((n_dp * 4,)), dma((n_dp,)), dma((n_dp,)), dma((n_dp,)),
            dma((TILES * 2 * PLANE,)), dma((TILES * 2 * PLANE,)),
            dma((TILES * PLANE,)), dma((TILES * PLANE,)),
            dma((n_dp,)), dma((n_dp,)), dma((2 * count,)), dma((2 * count,)), dma((2 * count,)), dma((2 * count,)),
            dma((2 * TILES + 2,)), dma,
        ],
        compiler_params=pltpu.CompilerParams(
            collective_id=0, has_side_effects=True, vmem_limit_bytes=55 << 20),
    )(features, labels, weight, noise)


def examples_split(features, labels, weight, noise):
    tok_rows = features.shape[0]
    feature_dim = features.shape[1]
    class_shard = weight.shape[1]
    groups = lax.axis_size("dp") // CSPLIT
    row_block = feature_dim // groups
    col_block = class_shard // CSPLIT
    slot_count = groups * CSPLIT
    feature_slots = jnp.broadcast_to(
        features.reshape(tok_rows, groups, 1, row_block), (tok_rows, groups, CSPLIT, row_block)
    ).reshape(tok_rows, slot_count, row_block)
    logits = jnp.dot(
        features,
        lax.all_gather(weight, "dp", axis=0, tiled=True),
        preferred_element_type=jnp.float32,
    )
    offset = labels - lax.axis_index("cls") * class_shard
    label_hit = lax.broadcasted_iota(jnp.int32, (tok_rows, class_shard), 1) == offset[:, None]
    onehot = label_hit.astype(jnp.float32)
    local_max = jnp.max(logits, axis=1)
    exponent = jnp.exp(logits - local_max[:, None])
    row_total = jnp.sum(exponent, axis=1)
    row_square = jnp.sum(exponent * exponent, axis=1)
    picked = jnp.sum(onehot * logits, axis=1)
    global_max = lax.pmax(local_max, "cls")
    rescale = jnp.exp(local_max - global_max)
    row_total, row_square, picked = lax.psum(
        (row_total * rescale, row_square * rescale * rescale, picked), "cls"
    )
    softmax = exponent * (jnp.exp(local_max - global_max) / row_total)[:, None]
    label_prob = jnp.exp(picked - global_max) / row_total
    spread = row_square / (row_total * row_total) - 2.0 * label_prob + 1.0
    energy = jnp.sum(jnp.square(features.astype(jnp.float32)), axis=1)
    factor = CLIP_NORM * lax.rsqrt(jnp.maximum(energy * spread, CLIP_NORM * CLIP_NORM))
    weighted = (factor[:, None] * (softmax - onehot)).astype(jnp.bfloat16)
    coef_slots = jnp.broadcast_to(
        weighted.reshape(tok_rows, 1, CSPLIT, col_block), (tok_rows, groups, CSPLIT, col_block)
    ).reshape(tok_rows, slot_count, col_block)
    feature_recv, coef_recv = (
        lax.all_to_all(feature_slots, "dp", split_axis=1, concat_axis=1, tiled=True),
        lax.all_to_all(coef_slots, "dp", split_axis=1, concat_axis=1, tiled=True),
    )
    grad_block = lax.dot_general(
        feature_recv, coef_recv, (((0, 1), (0, 1)), ((), ())), preferred_element_type=jnp.float32
    )
    return (grad_block + NOISE_STD * noise[0, 0]).reshape(noise.shape)


def on_device(features, labels, weight, noise):
    n_dp = lax.axis_size("dp")
    n_cls = lax.axis_size("cls")
    if n_dp != 2 * CSPLIT or n_cls != 2:
        return examples_split(features, labels, weight, noise)
    half = features.shape[0] // 2
    row_block = features.shape[1] // (n_dp // CSPLIT)
    col_block = weight.shape[1] // CSPLIT
    grad = head(features, labels.reshape(1, 2 * half), weight, noise[0, 0], n_dp, n_cls, row_block, col_block)
    return grad.reshape(noise.shape)


def solution(mesh):
    placed = (P("dp", None), P("dp"), P("dp", "cls"), P("dp", "cls", None, None))
    return jax.shard_map(
        on_device, mesh=mesh, in_specs=placed, out_specs=P("dp", "cls", None, None), check_vma=False
    )
```

```python
import functools

import jax
import jax.numpy as jnp
from jax import lax
from jax.experimental import pallas as pl
from jax.experimental.pallas import tpu as pltpu
from jax.sharding import PartitionSpec as P

CSPLIT = 8
CLIP_NORM = 40.0
NOISE_STD = 0.4
TILES = 4
PARTS = 2
PLANE = 4
LANES = 128
MESH = pl.DeviceIdType.MESH


def head_kernel(n_dp, n_cls, feat_ref, label_ref, weight_ref, noise_ref, out_ref,
                feats, turned_feats, wcols, wstage, exps, noise_buf, coefs, sides, label_cols, marks, maxima, early,
                stats, all_stats, finals, all_finals,
                fsend, frecv, bsend, brecv, psend, precv, zsend, zrecv, lsend, lrecv, tsend, trecv, gsend, grecv,
                local_sem, noise_sem):
    f32 = jnp.float32
    me = lax.axis_index("dp")
    cls = lax.axis_index("cls")
    sibling = 1 - cls
    stages = 4
    half, depth = feats.shape[2:]
    width = exps.shape[-1]
    cols = TILES * width
    last = TILES - 1
    row_block = turned_feats.shape[0]
    count = CSPLIT * n_cls
    place = me % CSPLIT * n_cls + cls
    level = me // PLANE
    spot = me % PLANE

    bit_step = [(1 << b) * (1 - 2 * ((me // (1 << b)) % 2)) for b in range(stages)]

    def flip(mask):
        return sum(bit_step[b] for b in range(stages) if mask >> b & 1)

    hops = sorted(range(1, count), key=lambda hop: (-(hop >> 1).bit_count(), hop))
    core_step = 1 - 2 * cls

    def group_peer(hop):
        return (me + flip(hop >> 1), cls + (hop & 1) * core_step)

    def peer_place(hop):
        return place + flip(hop >> 1) * n_cls + (hop & 1) * core_step

    barrier = pltpu.get_barrier_semaphore()
    crossed = [hop for hop in hops if hop & 1]
    for mask in sorted(range(1, n_dp), key=lambda mask: -((mask >> 2) + (mask & 3).bit_count())):
        pl.semaphore_signal(barrier, inc=1, device_id=(me + flip(mask), cls), device_id_type=MESH)
    for hop in crossed:
        pl.semaphore_signal(barrier, inc=1, device_id=group_peer(hop), device_id_type=MESH)
    pl.semaphore_wait(barrier, n_dp - 1 + len(crossed))

    def stage_steps(which):
        return [bit_step[3], bit_step[2],
                bit_step[1] * (1 - which) + bit_step[0] * which,
                bit_step[0] * (1 - which) + bit_step[1] * which]

    steps = stage_steps(cls)
    sib_steps = stage_steps(sibling)

    def origin(mask, table):
        there = me
        for s in range(stages):
            if mask >> s & 1:
                there = there + table[s]
        return there

    sends = []

    def push(source, target, out_sem, in_sem, device):
        copy = pltpu.make_async_remote_copy(
            src_ref=source, dst_ref=target, send_sem=out_sem, recv_sem=in_sem,
            device_id=device, device_id_type=MESH,
        )
        copy.start()
        return copy

    def arrived(ref, sem):
        pltpu.make_async_remote_copy(
            src_ref=ref, dst_ref=ref, send_sem=sem, recv_sem=sem,
            device_id=(me, sibling), device_id_type=MESH,
        ).wait_recv()

    def left(ref, sem):
        pltpu.make_async_remote_copy(
            src_ref=ref, dst_ref=ref, send_sem=sem, recv_sem=sem,
            device_id=(me, sibling), device_id_type=MESH,
        ).wait_send()

    own_half = feat_ref.at[pl.ds(pl.multiple_of(cls * half, half), half)]

    def feat_forward(mask, first, last):
        source = feats.at[cls, origin(mask, steps)] if mask else own_half
        for s in range(max(mask.bit_length(), first), last):
            sends.append(push(source, feats.at[cls, origin(mask, steps)], fsend.at[mask * stages + s],
                              frecv.at[mask | 1 << s], (me + steps[s], cls)))

    def feat_share(mask):
        block = feats.at[cls, origin(mask, steps)]
        sends.append(push(block, block, bsend.at[mask], brecv.at[mask], (me, sibling)))

    def feat_step(mask):
        arrived(feats.at[cls, origin(mask, steps)], frecv.at[mask])
        feat_forward(mask, 0, stages)
        feat_share(mask)

    parity = level % 2

    def block_cols(side, there, c):
        return pl.ds(pl.multiple_of((side * PLANE + there) * cols + c * width, LANES), width)

    def plane_send(c):
        for r in range(1, PLANE):
            peer = me + flip(r)
            at = c * 2 * PLANE + r * 2
            sends.append(push(weight_ref.at[:, block_cols(parity, peer % PLANE, c)], wcols.at[c, me],
                              psend.at[at], precv.at[at], (peer, cls)))
            sends.append(push(weight_ref.at[:, block_cols(1 - parity, peer % PLANE, c)], wstage.at[c, spot],
                              psend.at[at + 1], precv.at[at + 1], (peer, cls)))

    def plane_of(where):
        return pl.ds(pl.multiple_of(where * PLANE, PLANE), PLANE)

    def column_send(c):
        for r in range(1, PLANE):
            at = c * 2 * PLANE + r * 2
            arrived(wcols.at[c, me + flip(r)], precv.at[at])
            arrived(wstage.at[c, (me + flip(r)) % PLANE], precv.at[at + 1])
        for copy in keep[c]:
            copy.wait()
        block = wcols.at[c, plane_of(level)]
        for m in (2, 3, 1):
            at = c * PLANE + m
            push(block if m == 2 else wstage.at[c], block, zsend.at[at], zrecv.at[at], (me + flip(m * PLANE), cls))

    def sent(c):
        for m in range(1, PLANE):
            left(wstage.at[c], zsend.at[c * PLANE + m])

    feat_forward(0, 0, 2)
    plane_send(0)
    plane_send(1)
    keep = [[pltpu.make_async_copy(weight_ref.at[:, block_cols(parity, spot, c)], wcols.at[c, me],
                                   local_sem.at[2 * c]),
             pltpu.make_async_copy(weight_ref.at[:, block_cols(1 - parity, spot, c)], wstage.at[c, spot],
                                   local_sem.at[2 * c + 1])] for c in range(TILES)]
    own_feats = [pltpu.make_async_copy(feat_ref.at[pl.ds(h * half, half)], feats.at[h, me],
                                       local_sem.at[2 * TILES + h]) for h in range(2)]
    for copy in sum(keep, own_feats):
        copy.start()
    noise_copy = pltpu.make_async_copy(noise_ref, noise_buf, noise_sem)
    sides[me, :, 0:2 * half] = label_ref[...]
    for hop in range(1, n_dp):
        sends.append(push(sides.at[me], sides.at[me], lsend.at[hop], lrecv.at[hop], (me + flip(hop), cls)))

    feat_forward(0, 2, stages)
    column_send(0)
    for mask in (4, 8, 12):
        feat_step(mask)
    column_send(1)
    plane_send(2)
    for mask in (2, 6, 10, 14, 1, 5, 9, 13):
        feat_step(mask)
    noise_copy.start()
    sent(0)
    column_send(2)
    plane_send(3)
    for mask in (3, 7, 11, 15):
        feat_step(mask)
    sent(1)
    column_send(3)
    for mask in range(1, 16):
        arrived(feats.at[sibling, origin(mask, sib_steps)], brecv.at[mask])

    for hop in range(1, n_dp):
        arrived(sides.at[me + flip(hop)], lrecv.at[hop])
    for copy in own_feats:
        copy.wait()

    rows = jnp.concatenate([sides[i] for i in range(n_dp)], axis=0).astype(f32)
    rows = jnp.concatenate([rows, jnp.zeros((LANES - n_dp, 2 * LANES), f32)], axis=0).T
    for h in range(2):
        label_cols[h] = rows[h * half:(h + 1) * half]

    first_row = pl.multiple_of(me // CSPLIT * row_block, row_block)
    quad = LANES // 32

    def turn_body(t, carry):
        h, k = t // (n_dp // quad), t % (n_dp // quad)
        part = feats[h, pl.ds(k * quad, quad), :, pl.ds(first_row, row_block)].reshape(quad * half, row_block)
        turned_feats[:, pl.ds(pl.multiple_of(t * quad * half, LANES), quad * half)] = part.T
        return carry

    lax.fori_loop(0, 2 * n_dp // quad, turn_body, 0)

    lane = lax.broadcasted_iota(jnp.int32, (half, LANES), 1)
    energy_cols = jnp.zeros((half, LANES), f32)
    for h in range(2):
        value = feats[h, place].astype(f32)
        energy_cols = jnp.where(lane == h, jnp.sum(value * value, axis=1, keepdims=True), energy_cols)
    energy_rows = jnp.concatenate([energy_cols, jnp.zeros((LANES - half, LANES), f32)], axis=0).T

    base = cls * (CSPLIT * cols) + me % CSPLIT * cols

    def hits(labels, c):
        offset = labels.astype(jnp.int32) - (base + c * width)
        return lax.broadcasted_iota(jnp.int32, (half, width), 1) == offset

    def observe(logits, c, h, blocks, held):
        for k, i in enumerate(blocks):
            part = logits[k * half:(k + 1) * half]
            top = jnp.max(part, axis=1, keepdims=True)
            exponent = jnp.exp(part - top)
            exps[c, h, i] = exponent
            total = jnp.sum(exponent, axis=1, keepdims=True)
            square = jnp.sum(exponent * exponent, axis=1, keepdims=True)
            hit = hits(label_cols[h, :, i:i + 1], c)
            picked = jnp.sum(jnp.where(hit, exponent, 0.0), axis=1, keepdims=True)
            for s, value in enumerate((top, total, square, picked)):
                held = jnp.where(lane == s * n_dp + i, value, held)
        return held

    def measure(logits, c, h):
        marks[c, h] = observe(logits, c, h, range(n_dp), jnp.zeros((half, LANES), f32))

    def take(block, c, m):
        arrived(block.at[plane_of((me + flip(m * PLANE)) // PLANE)], zrecv.at[c * PLANE + m])

    def whole_dot(h, block):
        return jnp.dot(feats[h].reshape(n_dp * half, depth), block[...].reshape(depth, block.shape[-1]),
                       preferred_element_type=f32)

    def chunk_body(c, carry):
        block = wcols.at[c]

        for m in range(1, PLANE):
            take(block, c, m)

        def half_body(h, inner):
            measure(whole_dot(h, block), c, h)
            return inner

        return lax.fori_loop(0, 2, half_body, carry)

    lax.fori_loop(0, TILES - 1, chunk_body, 0)

    pad = jnp.zeros((LANES - half, LANES), f32)

    def turned_marks(c, h):
        turned = jnp.concatenate([marks[c, h], pad], axis=0).T
        maxima[c, h] = turned[0:n_dp]
        return [turned[s * n_dp:(s + 1) * n_dp] for s in range(4)]

    def merged(parts):
        top = functools.reduce(jnp.maximum, [part[0] for part in parts])
        fades = [jnp.exp(part[0] - top) for part in parts]
        return [top] + [sum(part[s] * (f * f if s == 2 else f) for part, f in zip(parts, fades)) for s in range(1, 4)]

    side = me // CSPLIT

    team = n_dp // PARTS

    def part_dot(h, g, which):
        first = pl.multiple_of(which * row_block, row_block)
        return jnp.dot(
            feats[h, pl.ds(g * team, team), :, pl.ds(first, row_block)].reshape(team * half, row_block),
            wcols[last, pl.ds(which * CSPLIT, CSPLIT)].reshape(row_block, width),
            preferred_element_type=f32)

    take(wcols.at[last], last, 1)

    def near_body(k, carry):
        out_ref[0:team * half, pl.ds(pl.multiple_of(k * width, width), width)] = part_dot(k // PARTS, k % PARTS, side)
        return carry

    lax.fori_loop(0, 2 * PARTS, near_body, 0)
    sent(last - 1)
    for copy in sends:
        copy.wait_send()
    for h in range(2):
        for s, row in enumerate(merged([turned_marks(c, h) for c in range(last)])):
            early[h, s] = row
    take(wcols.at[last], last, 2)
    take(wcols.at[last], last, 3)

    def join(h):
        rows = merged([[early[h, s] for s in range(4)], turned_marks(last, h)])
        for s in range(4):
            for i in range(n_dp):
                stats[h, i, s:s + 1, :] = rows[s][i:i + 1]
        for hop in hops:
            push(stats.at[h, peer_place(hop)], all_stats.at[h, place], tsend.at[h * count + hop],
                 trecv.at[h * count + hop], group_peer(hop))
        all_stats[h, place] = stats[h, place]

    def settle(h):
        for hop in hops:
            arrived(all_stats.at[h, peer_place(hop)], trecv.at[h * count + hop])
        tops, totals, squares, picks = (all_stats[h, :, s, :] for s in range(4))
        row_max = jnp.max(tops, axis=0, keepdims=True)
        fade = jnp.exp(tops - row_max)
        row_total = jnp.sum(totals * fade, axis=0, keepdims=True)
        row_square = jnp.sum(squares * fade * fade, axis=0, keepdims=True)
        picked = jnp.sum(picks * fade, axis=0, keepdims=True)
        inverse = 1.0 / row_total
        spread = row_square * inverse * inverse - 2.0 * picked * inverse + 1.0
        energy = energy_rows[h:h + 1]
        factor = CLIP_NORM * lax.rsqrt(jnp.maximum(energy * spread, CLIP_NORM * CLIP_NORM))
        finals[h, 0:1, :] = row_max
        finals[h, 1:2, :] = factor * inverse
        finals[h, 2:3, :] = factor
        finals[h, 3:4, :] = factor
        for hop in hops:
            push(finals.at[h], all_finals.at[h, place], gsend.at[h * count + hop],
                 grecv.at[h * count + hop], group_peer(hop))
        all_finals[h, place] = finals[h]

    fill = jnp.zeros((LANES - (TILES + 1) * n_dp, LANES), f32)

    def scales(h):
        for hop in hops:
            arrived(all_finals.at[h, peer_place(hop)], grecv.at[h * count + hop])
        row_max, share, factor = (all_finals[h, :, s, :] for s in range(3))
        scale = [share * jnp.exp(maxima[c, h] - row_max) for c in range(TILES)]
        marks[0, h] = jnp.concatenate(scale + [factor, fill], axis=0).T[0:half]

    def coefficients(h, c):
        for i in range(n_dp):
            hit = hits(label_cols[h, :, i:i + 1], c)
            scale = marks[0, h, :, c * n_dp + i:c * n_dp + i + 1]
            factor = marks[0, h, :, last * n_dp + n_dp + i:last * n_dp + n_dp + i + 1]
            value = exps[c, h, i] * scale - jnp.where(hit, factor, 0.0)
            coefs[c % 2, i * half:(i + 1) * half, :] = value.astype(coefs.dtype)

    def far_body(h, carry):
        logits = [
            out_ref[0:team * half, pl.ds(pl.multiple_of((h * PARTS + g) * width, width), width)]
            + part_dot(h, g, 1 - side) for g in range(PARTS)]
        held = jnp.zeros((half, LANES), f32)
        for g in range(PARTS):
            held = observe(logits[g], last, h, range(g * team, (g + 1) * team), held)
        marks[last, h] = held
        join(h)
        return carry

    lax.fori_loop(0, 2, far_body, 0)
    settle(0)
    settle(1)
    noise_copy.wait()
    scales(0)
    coefficients(0, 0)
    for h in range(2):
        for c in range(TILES):
            if c + 1 < TILES:
                coefficients(h, c + 1)
            elif h == 0:
                scales(1)
                coefficients(1, 0)
            at = slice(c * width, (c + 1) * width)
            begin = h * n_dp * half
            grad = jnp.dot(turned_feats[:, begin:begin + n_dp * half], coefs[c % 2], preferred_element_type=f32)
            out_ref[:, at] = grad + (out_ref[:, at] if h else NOISE_STD * noise_buf[:, at])
    sent(last)
    for h in range(2):
        for hop in range(1, count):
            left(stats.at[h, 0], tsend.at[h * count + hop])
            left(finals.at[h], gsend.at[h * count + hop])


def head(features, labels, weight, noise, n_dp, n_cls, row_block, col_block):
    rows, depth = features.shape
    half = rows // 2
    count = CSPLIT * n_cls
    width = col_block // TILES
    depth_block = weight.shape[0]
    anywhere = pl.BlockSpec(memory_space=pl.ANY)
    dma = pltpu.SemaphoreType.DMA
    f32 = jnp.float32
    bf16 = jnp.bfloat16
    return pl.pallas_call(
        functools.partial(head_kernel, n_dp, n_cls),
        out_shape=pltpu.VMEM((row_block, col_block), f32),
        in_specs=[anywhere, pl.BlockSpec(memory_space=pltpu.VMEM), anywhere, anywhere],
        out_specs=pl.BlockSpec(memory_space=pltpu.VMEM),
        scratch_shapes=[
            pltpu.VMEM((2, n_dp, half, depth), bf16),
            pltpu.VMEM((row_block, n_dp * rows), bf16),
            pltpu.VMEM((TILES, n_dp, depth_block, width), bf16),
            pltpu.VMEM((TILES, PLANE, depth_block, width), bf16),
            pltpu.VMEM((TILES, 2, n_dp, half, width), f32),
            pltpu.VMEM((row_block, col_block), f32),
            pltpu.VMEM((2, n_dp * half, width), bf16),
            pltpu.VMEM((n_dp, 1, 2 * LANES), jnp.int32),
            pltpu.VMEM((2, half, LANES), f32),
            pltpu.VMEM((TILES, 2, half, LANES), f32),
            pltpu.VMEM((TILES, 2, n_dp, LANES), f32),
            pltpu.VMEM((2, 4, n_dp, LANES), f32),
            pltpu.VMEM((2, count, 4, LANES), f32),
            pltpu.VMEM((2, count, 4, LANES), f32),
            pltpu.VMEM((2, 4, LANES), f32),
            pltpu.VMEM((2, count, 4, LANES), f32),
            dma((n_dp * 4,)), dma((n_dp,)), dma((n_dp,)), dma((n_dp,)),
            dma((TILES * 2 * PLANE,)), dma((TILES * 2 * PLANE,)),
            dma((TILES * PLANE,)), dma((TILES * PLANE,)),
            dma((n_dp,)), dma((n_dp,)), dma((2 * count,)), dma((2 * count,)), dma((2 * count,)), dma((2 * count,)),
            dma((2 * TILES + 2,)), dma,
        ],
        compiler_params=pltpu.CompilerParams(
            collective_id=0, has_side_effects=True, vmem_limit_bytes=55 << 20),
    )(features, labels, weight, noise)


def examples_split(features, labels, weight, noise):
    tok_rows = features.shape[0]
    feature_dim = features.shape[1]
    class_shard = weight.shape[1]
    groups = lax.axis_size("dp") // CSPLIT
    row_block = feature_dim // groups
    col_block = class_shard // CSPLIT
    slot_count = groups * CSPLIT
    feature_slots = jnp.broadcast_to(
        features.reshape(tok_rows, groups, 1, row_block), (tok_rows, groups, CSPLIT, row_block)
    ).reshape(tok_rows, slot_count, row_block)
    logits = jnp.dot(
        features,
        lax.all_gather(weight, "dp", axis=0, tiled=True),
        preferred_element_type=jnp.float32,
    )
    offset = labels - lax.axis_index("cls") * class_shard
    label_hit = lax.broadcasted_iota(jnp.int32, (tok_rows, class_shard), 1) == offset[:, None]
    onehot = label_hit.astype(jnp.float32)
    local_max = jnp.max(logits, axis=1)
    exponent = jnp.exp(logits - local_max[:, None])
    row_total = jnp.sum(exponent, axis=1)
    row_square = jnp.sum(exponent * exponent, axis=1)
    picked = jnp.sum(onehot * logits, axis=1)
    global_max = lax.pmax(local_max, "cls")
    rescale = jnp.exp(local_max - global_max)
    row_total, row_square, picked = lax.psum(
        (row_total * rescale, row_square * rescale * rescale, picked), "cls"
    )
    softmax = exponent * (jnp.exp(local_max - global_max) / row_total)[:, None]
    label_prob = jnp.exp(picked - global_max) / row_total
    spread = row_square / (row_total * row_total) - 2.0 * label_prob + 1.0
    energy = jnp.sum(jnp.square(features.astype(jnp.float32)), axis=1)
    factor = CLIP_NORM * lax.rsqrt(jnp.maximum(energy * spread, CLIP_NORM * CLIP_NORM))
    weighted = (factor[:, None] * (softmax - onehot)).astype(jnp.bfloat16)
    coef_slots = jnp.broadcast_to(
        weighted.reshape(tok_rows, 1, CSPLIT, col_block), (tok_rows, groups, CSPLIT, col_block)
    ).reshape(tok_rows, slot_count, col_block)
    feature_recv, coef_recv = (
        lax.all_to_all(feature_slots, "dp", split_axis=1, concat_axis=1, tiled=True),
        lax.all_to_all(coef_slots, "dp", split_axis=1, concat_axis=1, tiled=True),
    )
    grad_block = lax.dot_general(
        feature_recv, coef_recv, (((0, 1), (0, 1)), ((), ())), preferred_element_type=jnp.float32
    )
    return (grad_block + NOISE_STD * noise[0, 0]).reshape(noise.shape)


def on_device(features, labels, weight, noise):
    n_dp = lax.axis_size("dp")
    n_cls = lax.axis_size("cls")
    if n_dp != 2 * CSPLIT or n_cls != 2:
        return examples_split(features, labels, weight, noise)
    half = features.shape[0] // 2
    row_block = features.shape[1] // (n_dp // CSPLIT)
    col_block = weight.shape[1] // CSPLIT
    grad = head(features, labels.reshape(1, 2 * half), weight, noise[0, 0], n_dp, n_cls, row_block, col_block)
    return grad.reshape(noise.shape)


def solution(mesh):
    placed = (P("dp", None), P("dp"), P("dp", "cls"), P("dp", "cls", None, None))
    return jax.shard_map(
        on_device, mesh=mesh, in_specs=placed, out_specs=P("dp", "cls", None, None), check_vma=False
    )
```
